32 devices in a mesh: groups: 2 (over y), seq: 8 (over z, core), heads: 2 (over x), sub: 1.
Axes of the slice: x: 2, y: 2, z: 4, core: 2. Of those that a mesh axis runs over, the one named last changes fastest.
Arguments:
- video_q: bfloat16 [5120, 2048], P(('groups', 'seq'), ('heads', 'sub')), parts along dimension 0, may hold values from -10 to 10
- video_cross_keys: bfloat16 [5120, 2048], P(('groups', 'seq'), ('heads', 'sub')), parts along dimension 0, may hold values from -10 to 10
- video_v: bfloat16 [5120, 2048], P(('groups', 'seq'), ('heads', 'sub')), parts along dimension 0, may hold values from -6 to 6
- audio_q: bfloat16 [1280, 2048], P(('groups', 'seq'), ('heads', 'sub')), parts along dimension 0, may hold values from -10 to 10
- audio_k: bfloat16 [1280, 2048], P(('groups', 'seq'), ('heads', 'sub')), parts along dimension 0, may hold values from -10 to 10
- audio_v: bfloat16 [1280, 2048], P(('groups', 'seq'), ('heads', 'sub')), parts along dimension 0, may hold values from -6 to 6
- audio_self_q: bfloat16 [1280, 2048], P(('groups', 'seq'), ('heads', 'sub')), parts along dimension 0, may hold values from -10 to 10
- audio_self_keys: bfloat16 [1280, 2048], P(('groups', 'seq'), ('heads', 'sub')), parts along dimension 0, may hold values from -10 to 10
- audio_self_v: bfloat16 [1280, 2048], P(('groups', 'seq'), ('heads', 'sub')), parts along dimension 0, may hold values from -6 to 6
- video_counts: int32 [16], P('groups'), parts along dimension 0, may hold values from 1 to 320, 2048 in all
- audio_counts: int32 [16], P('groups'), parts along dimension 0, may hold values from 1 to 80, 512 in all
- window_start: int32 [16], P('groups'), parts along dimension 0, may hold values from 0 to 3, as said below
- window_end: int32 [16], P('groups'), parts along dimension 0, may hold values from 1 to 4, as said below
Outputs:
- video_out: bfloat16 [5120, 2048], P(('groups', 'seq'), ('heads', 'sub')), parts along dimension 0
- audio_out: bfloat16 [1280, 2048], P(('groups', 'seq'), ('heads', 'sub')), parts along dimension 0
The draws below stay inside these ranges and needn't reach their ends.
There are 2 independent parts, one for each index of `groups`. The reference program is written for one: setup_inputs(seed, part) draws one part's arguments, and reference() takes and returns one part's arrays. A program takes and returns all parts, laid end to end along the dimension named above; each array names one. Nothing has to cross between parts.
Inputs may be any that keep to these rules, and one draw needn't show every extreme that they name: `video_counts`: the live tokens of each seq index's block of slots come first in it. `audio_counts`: the live tokens of each seq index's block of slots come first in it. window_start[f] is f // 2 or one less, never below 0, except for the frames with f // 2 = 2, whose window holds all 4 blocks. window_end[f] is f // 2 plus one or two, never above 4, except for the frames whose window holds all blocks.
All inputs are finite; a program needn't handle non-finite values.
Results may differ from the reference program's by a relative error of at most 0.0085.
Values may be sent and summed in bfloat16 or wider, within the bound.
A program may use at most 64 MiB of HBM per device.

```python
import math
import jax
import jax.numpy as jnp
import numpy as np
from jax import lax

HEADS = 32
HD = 64
FRAME_TOKENS = 256
AUDIO_WIN_BLOCK = 128
VCAP = 320
ACAP = 80
VTOK = 2048
LIVE_AUDIO_TOKEN = 512
VSLOTS = 2560
ASLOTS = 640
NF = 8
NAB = 4
N_SEQ = 8


def drawn(key, tag, row_count, asking):
    columns = HEADS * HD
    spread = 2.5 if asking == 1 else 1.0
    values = jnp.clip(spread * jax.random.normal(jax.random.fold_in(key, tag * 10 + asking), (row_count, columns), jnp.float32), -10.0, 10.0)
    return values.astype(jnp.bfloat16)


def draw_video_q(key, part):
    return drawn(key, 1, VSLOTS, 1)


def draw_audio_k(key, part):
    return drawn(key, 1, ASLOTS, 0)


def draw_audio_q(key, part):
    return drawn(key, 2, ASLOTS, 1)


def draw_video_cross_keys(key, part):
    return drawn(key, 2, VSLOTS, 0)


def draw_audio_self_q(key, part):
    return drawn(key, 3, ASLOTS, 1)


def draw_audio_self_keys(key, part):
    return drawn(key, 3, ASLOTS, 0)


def frame_windows(key):
    ratio = NF // NAB
    frames = jnp.arange(NF, dtype=jnp.int32)
    center = frames // ratio
    below = jax.random.randint(jax.random.fold_in(key, 71), (NF,), 0, 2, dtype=jnp.int32)
    above = jax.random.randint(jax.random.fold_in(key, 72), (NF,), 0, 2, dtype=jnp.int32)
    forced = frames == (NAB // 2 - 1) * ratio
    below = jnp.where(forced, 1, below)
    above = jnp.where(forced, 1, above)
    wide = center == NAB // 2
    first = jnp.where(wide, 0, jnp.maximum(center - below, 0)).astype(jnp.int32)
    final = jnp.where(wide, NAB, jnp.minimum(center + 1 + above, NAB)).astype(jnp.int32)
    return (first, final)


def draw_window_start(key, part):
    return frame_windows(key)[0]


def draw_window_end(key, part):
    return frame_windows(key)[1]


def level_of(own_key, shape, shards, smallest, largest):
    loudness, own = 1.0, jax.random.fold_in(own_key, 6)
    for dim, shards_of in shards:
        heights = jnp.exp(jax.random.uniform(jax.random.fold_in(own, dim), (shards_of,), jnp.float32, smallest / len(shards), largest / len(shards)))
        loudness = loudness * jnp.repeat(heights, shape[dim] // shards_of).reshape([-1 if axis == dim else 1 for axis in range(len(shape))])
    return loudness


def profile(count, total, most, lean):
    loads = [(1 << 20) // math.isqrt(standing ** lean) + 1 for standing in range(2, count + 1)]
    rest, given = total - most - (count - 1), [1] * (count - 1)
    while rest > 0:
        free = [i for i in range(count - 1) if given[i] < most]
        whole, budget = sum([loads[i] for i in free]), rest
        for i in free:
            addition = min(most - given[i], max(1, budget * loads[i] // whole), rest)
            given[i] = given[i] + addition
            rest = rest - addition
    return np.array([most] + given)


def ragged_sizes(key, number_of, total, bound, skew):
    if number_of == 2:
        one = jax.random.randint(key, (), max(1, total - bound), min(bound, total - 1) + 1)
        return jnp.stack([one, total - one])
    tallies = jnp.asarray(profile(number_of, total, bound, skew), jnp.int32)
    couples = (number_of - 1) // 2
    source_of, sink = tallies[1:1 + 2 * couples:2], tallies[2:2 + 2 * couples:2]
    margin = jnp.minimum(source_of - 1, bound - sink)
    shifted = jax.random.randint(jax.random.fold_in(key, 1), (couples,), 0, 1 << 20) % (margin + 1)
    tallies = tallies.at[1:1 + 2 * couples:2].set(source_of - shifted).at[2:2 + 2 * couples:2].set(sink + shifted)
    return tallies[jax.random.permutation(jax.random.fold_in(key, 2), number_of)]


def scatter_about(stream_key, dims, width, most, shards=(), kind=jnp.bfloat16):
    loudness = level_of(stream_key, dims, shards, -0.22, 0.18) if shards else 1.0
    result = jax.random.normal(stream_key, dims, jnp.float32) * width * loudness
    return jnp.minimum(jnp.maximum(result, -most), most).astype(kind)


def setup_inputs(seed: int = 0, part: int = 0) -> dict:
    splits = jax.random.split(jax.random.key(seed), 14)
    own_keys = jax.random.split(jax.random.fold_in(splits[13], part), 14)
    video_q = draw_video_q(jax.random.fold_in(jax.random.fold_in(splits[13], part), 71), part)
    video_cross_keys = draw_video_cross_keys(jax.random.fold_in(jax.random.fold_in(splits[13], part), 71), part)
    video_v = scatter_about(own_keys[2], (VSLOTS, HEADS * HD), 1.0, 6.0, ((0, 8), (1, 2)))
    audio_q = draw_audio_q(jax.random.fold_in(jax.random.fold_in(splits[13], part), 71), part)
    audio_k = draw_audio_k(jax.random.fold_in(jax.random.fold_in(splits[13], part), 71), part)
    audio_v = scatter_about(own_keys[5], (ASLOTS, HEADS * HD), 1.0, 6.0, ((0, 8), (1, 2)))
    audio_self_q = draw_audio_self_q(jax.random.fold_in(jax.random.fold_in(splits[13], part), 71), part)
    audio_self_keys = draw_audio_self_keys(jax.random.fold_in(jax.random.fold_in(splits[13], part), 71), part)
    audio_self_v = scatter_about(own_keys[8], (ASLOTS, HEADS * HD), 1.0, 6.0, ((0, 8), (1, 2)))
    video_counts = ragged_sizes(own_keys[9], N_SEQ, VTOK, VCAP, 2).astype(jnp.int32)
    audio_counts = ragged_sizes(own_keys[10], N_SEQ, LIVE_AUDIO_TOKEN, ACAP, 2).astype(jnp.int32)
    window_start = draw_window_start(jax.random.fold_in(jax.random.fold_in(splits[13], part), 71), part)
    window_end = draw_window_end(jax.random.fold_in(jax.random.fold_in(splits[13], part), 71), part)
    return {"video_q": video_q, "video_cross_keys": video_cross_keys, "video_v": video_v, "audio_q": audio_q, "audio_k": audio_k, "audio_v": audio_v, "audio_self_q": audio_self_q, "audio_self_keys": audio_self_keys, "audio_self_v": audio_self_v, "video_counts": video_counts, "audio_counts": audio_counts, "window_start": window_start, "window_end": window_end}


NEG = -1e30


def slot_of(counts, capacity, total):
    ends = jnp.cumsum(counts).astype(jnp.int32)
    starts = (ends - counts).astype(jnp.int32)
    places = jnp.arange(total, dtype=jnp.int32)
    owner = jnp.sum((ends[None, :] <= places[:, None]).astype(jnp.int32), axis=1).astype(jnp.int32)
    return (owner * capacity + places - starts[owner]).astype(jnp.int32)


def attend_pairs(query, key_rows, values, allowed):
    scores = jnp.einsum("qhd,khd->qhk", query.astype(jnp.float32), key_rows.astype(jnp.float32)) * (HD ** -0.5)
    scores = jnp.where(allowed[:, None, :], scores, NEG)
    highest = jnp.max(scores, axis=2, keepdims=True)
    weights = jnp.where(allowed[:, None, :], jnp.exp(scores - highest), 0.0)
    total = jnp.sum(weights, axis=2)
    rounded = lax.optimization_barrier(weights.astype(jnp.bfloat16)).astype(jnp.float32)
    mixed = jnp.einsum("qhk,khd->qhd", rounded, values.astype(jnp.float32))
    return mixed / total[:, :, None]


def reference(video_q, video_cross_keys, video_v, audio_q, audio_k, audio_v, audio_self_q, audio_self_keys, audio_self_v, video_counts, audio_counts, window_start, window_end):
    def head_count(array, slots):
        return array[slots].reshape(slots.shape[0], HEADS, HD)

    video_slot_table = slot_of(video_counts, VCAP, VTOK)
    audio_slot_table = slot_of(audio_counts, ACAP, LIVE_AUDIO_TOKEN)
    vquery = head_count(video_q, video_slot_table)
    video_key_rows = head_count(video_cross_keys, video_slot_table)
    vvalues = head_count(video_v, video_slot_table)
    aquery = head_count(audio_q, audio_slot_table)
    akeys = head_count(audio_k, audio_slot_table)
    avalues = head_count(audio_v, audio_slot_table)
    squery = head_count(audio_self_q, audio_slot_table)
    self_key_rows = head_count(audio_self_keys, audio_slot_table)
    self_value_rows = head_count(audio_self_v, audio_slot_table)
    audio_block_of = (jnp.arange(LIVE_AUDIO_TOKEN, dtype=jnp.int32) // AUDIO_WIN_BLOCK).astype(jnp.int32)

    def video_frame(frame):
        row_count = lax.dynamic_slice_in_dim(vquery, (frame * FRAME_TOKENS).astype(jnp.int32), FRAME_TOKENS, 0)
        inside = (audio_block_of >= window_start[frame]) & (audio_block_of < window_end[frame])
        return attend_pairs(row_count, akeys, avalues, jnp.broadcast_to(inside[None, :], (FRAME_TOKENS, LIVE_AUDIO_TOKEN)))

    video_result = lax.map(video_frame, jnp.arange(NF, dtype=jnp.int32)).reshape(VTOK, HEADS * HD)

    frame_of = (jnp.arange(VTOK, dtype=jnp.int32) // FRAME_TOKENS).astype(jnp.int32)
    key_first = window_start[frame_of]
    key_final = window_end[frame_of]
    row_step = AUDIO_WIN_BLOCK // 4

    def audio_rows(index):
        first_row = (index * row_step).astype(jnp.int32)
        row_count = lax.dynamic_slice_in_dim(aquery, first_row, row_step, 0)
        block = first_row // AUDIO_WIN_BLOCK
        inside = (key_first <= block) & (block < key_final)
        return attend_pairs(row_count, video_key_rows, vvalues, jnp.broadcast_to(inside[None, :], (row_step, VTOK)))

    cross = lax.map(audio_rows, jnp.arange(LIVE_AUDIO_TOKEN // row_step, dtype=jnp.int32)).reshape(LIVE_AUDIO_TOKEN, HEADS, HD)
    united = (squery.astype(jnp.float32) + cross).astype(jnp.bfloat16)

    def self_block(block):
        row_count = lax.dynamic_slice_in_dim(united, (block * AUDIO_WIN_BLOCK).astype(jnp.int32), AUDIO_WIN_BLOCK, 0)
        return attend_pairs(row_count, self_key_rows, self_value_rows, jnp.ones((AUDIO_WIN_BLOCK, LIVE_AUDIO_TOKEN), dtype=bool))

    own = lax.map(self_block, jnp.arange(NAB, dtype=jnp.int32)).reshape(LIVE_AUDIO_TOKEN, HEADS, HD)
    audio_result = (cross + own).astype(jnp.bfloat16).reshape(LIVE_AUDIO_TOKEN, HEADS * HD)
    video_out = jnp.zeros((VSLOTS, HEADS * HD), jnp.bfloat16).at[video_slot_table].set(video_result.astype(jnp.bfloat16))
    audio_out = jnp.zeros((ASLOTS, HEADS * HD), jnp.bfloat16).at[audio_slot_table].set(audio_result)
    return video_out, audio_out
```

```python
import functools
import math

import jax
import jax.numpy as jnp
from jax import lax
from jax.experimental import pallas as pl
from jax.experimental.pallas import tpu as pltpu
from jax.sharding import PartitionSpec as P

HD = 64
PAIR = 128
FRAME_TOKENS = 256
AUDIO_WIN_BLOCK = 128
NEG = -1e30
FAR = 1 << 20
SCALE = HD ** (-0.5) * math.log2(math.e)
MESH = pl.DeviceIdType.MESH
Q, K, V, SK, SV = range(5)


def kernel(
    n,
    frames,
    vcount,
    acount,
    wstart,
    wend,
    vq,
    vk,
    vv,
    aq,
    ak,
    av,
    sq,
    sk,
    sv,
    vout,
    aout,
    vqs,
    vks,
    vvs,
    sqs,
    gq,
    gk,
    gv,
    gsk,
    gsv,
    vbias,
    pacc,
    pst,
    sacc,
    racc,
    rst,
    local_sem,
    send_sem,
    recv_sem,
    psend,
    precv,
):
    me = lax.axis_index("seq")
    vslots, width = vqs.shape
    aslots = sqs.shape[0]
    pairs = width // PAIR
    total = n * aslots
    bufs = (gq, gk, gv, gsk, gsv)
    owns = (aq, ak, av, sk, sv)

    fetches = []
    for t in (Q, K, V, SK, SV):
        fetches.append(pltpu.make_async_copy(owns[t], bufs[t].at[me], local_sem.at[t]))
    for i, (a, b) in enumerate(((vk, vks), (vv, vvs), (vq, vqs), (sq, sqs))):
        fetches.append(pltpu.make_async_copy(a, b, local_sem.at[5 + i]))
    for f in fetches:
        f.start()

    has_left = me > 0
    has_right = me < n - 1
    barrier = pltpu.get_barrier_semaphore()

    @pl.when(has_left)
    def _():
        pl.semaphore_signal(barrier, inc=1, device_id={"seq": me - 1}, device_id_type=MESH)

    @pl.when(has_right)
    def _():
        pl.semaphore_signal(barrier, inc=1, device_id={"seq": me + 1}, device_id_type=MESH)

    @pl.when(jnp.logical_and(has_left, has_right))
    def _():
        pl.semaphore_wait(barrier, 2)

    @pl.when(jnp.logical_not(jnp.logical_and(has_left, has_right)))
    def _():
        pl.semaphore_wait(barrier, 1)

    def relay(t, d, r):
        source = me - r if d == 0 else me + r
        target = me + 1 if d == 0 else me - 1
        return pltpu.make_async_remote_copy(
            src_ref=bufs[t].at[source],
            dst_ref=bufs[t].at[source],
            send_sem=send_sem.at[t, d, r],
            recv_sem=recv_sem.at[t, d, r + 1],
            device_id={"seq": target},
            device_id_type=MESH,
        )

    def have(d, r):
        return me - r >= 0 if d == 0 else me + r <= n - 1

    def passes(d):
        return has_right if d == 0 else has_left

    def arrived(t, d, r):
        source = me - r if d == 0 else me + r
        pltpu.make_async_copy(
            bufs[t].at[source], bufs[t].at[source], recv_sem.at[t, d, r]
        ).wait()

    def forward(t, r, first=False):
        for d in (0, 1):

            @pl.when(have(d, r))
            def _():
                if not first:
                    arrived(t, d, r)

                @pl.when(passes(d))
                def _():
                    relay(t, d, r).start()

    def sent(t, r):
        for d in (0, 1):

            @pl.when(jnp.logical_and(have(d, r), passes(d)))
            def _():
                relay(t, d, r).wait_send()

    for t in (Q, K, V):
        fetches[t].wait()
        forward(t, 0, True)

    lane = lax.broadcasted_iota(jnp.int32, (1, PAIR), 1)
    low = lane < HD
    keep = (
        jnp.where(low, 1.0, 0.0).astype(jnp.bfloat16),
        jnp.where(low, 0.0, 1.0).astype(jnp.bfloat16),
    )

    def start_of(counts, index):
        at = jnp.int32(0)
        for s in range(n):
            at = at + jnp.where(s < index, counts[s], 0)
        return at

    def video_window(place):
        position = start_of(vcount, me) + place
        live = place < vcount[me]
        frame = position // FRAME_TOKENS
        first = jnp.full(place.shape, FAR, jnp.int32)
        final = jnp.zeros(place.shape, jnp.int32)
        for f in range(frames):
            here = jnp.logical_and(frame == f, live)
            first = jnp.where(here, wstart[f], first)
            final = jnp.where(here, wend[f], final)
        return first, final

    def weigh(query, key_rows, values, bias):
        score = (
            lax.dot_general(
                query, key_rows, (((1,), (1,)), ((), ())), preferred_element_type=jnp.float32
            )
            * SCALE
            + bias
        )
        top = jnp.max(score, axis=1, keepdims=True)
        weight = jnp.exp2(score - top)
        mass = jnp.sum(weight, axis=1, keepdims=True)
        mixed = jnp.dot(
            weight.astype(jnp.bfloat16), values, preferred_element_type=jnp.float32
        )
        return top, mass, mixed

    first_row, final_row = video_window(lax.broadcasted_iota(jnp.int32, (1, vslots), 1))
    video_place = lax.broadcasted_iota(jnp.int32, (vslots, 1), 0)
    first_col, final_col = video_window(video_place)
    audio_index = lax.broadcasted_iota(jnp.int32, (1, total), 1)
    audio_block = jnp.full((1, total), -1, jnp.int32)
    begin = jnp.int32(0)
    for s in range(n):
        place = audio_index - s * aslots
        here = jnp.logical_and(place >= 0, place < acount[s])
        audio_block = jnp.where(here, (begin + place) // AUDIO_WIN_BLOCK, audio_block)
        begin = begin + acount[s]
    vbias[...] = jnp.where(
        jnp.logical_and(first_col <= audio_block, audio_block < final_col), 0.0, NEG
    )
    self_bias = jnp.where(audio_block >= 0, 0.0, NEG)
    audio_place = lax.broadcasted_iota(jnp.int32, (aslots, 1), 0)

    def columns(p):
        return pl.ds(pl.multiple_of(p * PAIR, PAIR), PAIR)

    def audio_cross(j):
        block = jnp.where(
            audio_place < acount[j],
            (start_of(acount, j) + audio_place) // AUDIO_WIN_BLOCK,
            -1,
        )
        bias = jnp.where(
            jnp.logical_and(first_row <= block, block < final_row), 0.0, NEG
        )

        def step(p, stats):
            cols = columns(p)
            query = gq[j, :, cols]
            key_rows = vks[:, cols]
            values = vvs[:, cols]
            parts = []
            for h in (0, 1):
                top, mass, mixed = weigh(query * keep[h], key_rows, values, bias)
                stats = jnp.where(lane == 2 * p + h, top, stats)
                stats = jnp.where(lane == HD + 2 * p + h, mass, stats)
                parts.append(mixed)
            pacc[j, :, cols] = jnp.where(low, parts[0], parts[1])
            return stats

        pst[j] = lax.fori_loop(
            0, pairs, step, jnp.zeros((aslots, PAIR), jnp.float32), unroll=min(4, pairs)
        )

    fetches[5].wait()
    fetches[6].wait()

    def first_round(r, carry):
        @pl.when(r > 0)
        def _():
            for t in (Q, K, V):
                forward(t, r)

        @pl.when(have(0, r))
        def _():
            audio_cross(me - r)

        @pl.when(jnp.logical_and(have(1, r), r > 0))
        def _():
            audio_cross(me + r)

        return carry

    lax.fori_loop(0, n, first_round, 0)
    fetches[SK].wait()
    fetches[SV].wait()
    fetches[7].wait()
    fetches[8].wait()

    def merge(d, j):
        mine = pst[j]
        other = rst[d, j]
        top = jnp.maximum(mine, other)
        a = jnp.exp2(mine - top)
        b = jnp.exp2(other - top)
        mass = mine * pltpu.roll(a, HD, 1) + other * pltpu.roll(b, HD, 1)
        pst[j] = jnp.where(low, top, mass)
        for p in range(pairs):
            cols = pl.ds(p * PAIR, PAIR)
            wa = jnp.where(low, a[:, 2 * p : 2 * p + 1], a[:, 2 * p + 1 : 2 * p + 2])
            wb = jnp.where(low, b[:, 2 * p : 2 * p + 1], b[:, 2 * p + 1 : 2 * p + 2])
            pacc[j, :, cols] = pacc[j, :, cols] * wa + racc[d, j, :, cols].astype(
                jnp.float32
            ) * wb

    def pushes(d, j):
        target = me + 1 if d == 0 else me - 1
        return [
            pltpu.make_async_remote_copy(
                src_ref=src.at[j],
                dst_ref=dst.at[d, j],
                send_sem=psend.at[d, i, j],
                recv_sem=precv.at[d, i, j],
                device_id={"seq": target},
                device_id_type=MESH,
            )
            for i, (src, dst) in enumerate(((sacc, racc), (pst, rst)))
        ]

    def chain(d, step):
        lag = me if d == 0 else n - 1 - me
        j = n - 1 - step + me if d == 0 else step - (n - 1 - me)

        @pl.when(step >= lag)
        def _():
            @pl.when(passes(1 - d))
            def _():
                for i, dst in enumerate((racc, rst)):
                    pltpu.make_async_copy(
                        dst.at[d, j], dst.at[d, j], precv.at[d, i, j]
                    ).wait()
                merge(d, j)

            @pl.when(j != me)
            def _():
                sacc[j] = pacc[j].astype(jnp.bfloat16)
                for c in pushes(d, j):
                    c.start()

    video_live = video_place < vcount[me]
    chunk = 160 if vslots % 160 == 0 else vslots

    def video_pair(p, carry):
        cols = columns(p)
        key_rows = gk[:, :, cols].reshape(total, PAIR)
        values = gv[:, :, cols].reshape(total, PAIR)
        for c in range(vslots // chunk):
            rows = pl.ds(c * chunk, chunk)
            query = vqs[rows, cols]
            bias = vbias[rows, :]
            parts = []
            for h in (0, 1):
                top, mass, mixed = weigh(query * keep[h], key_rows, values, bias)
                parts.append(mixed / mass)
            result = jnp.where(low, parts[0], parts[1])
            live = video_live[c * chunk : (c + 1) * chunk]
            vout[rows, cols] = jnp.where(live, result, 0.0).astype(jnp.bfloat16)
        return carry

    per_step = -(-pairs // n)

    def second_round(r, carry):
        @pl.when(r == 0)
        def _():
            forward(SK, 0, True)
            forward(SV, 0, True)

        @pl.when(r > 0)
        def _():
            forward(SK, r)
            forward(SV, r)

        chain(0, r)
        chain(1, r)
        for i in range(per_step):

            @pl.when(r * per_step + i < pairs)
            def _():
                video_pair(r * per_step + i, 0)

        return carry

    lax.fori_loop(0, n, second_round, 0)

    audio_live = audio_place < acount[me]
    stats = pst[me]
    for p in range(pairs):
        cols = pl.ds(p * PAIR, PAIR)
        mass = jnp.where(
            low,
            stats[:, HD + 2 * p : HD + 2 * p + 1],
            stats[:, HD + 2 * p + 1 : HD + 2 * p + 2],
        )
        cross = jnp.where(audio_live, pacc[me, :, cols] / mass, 0.0)
        united = (sqs[:, cols].astype(jnp.float32) + cross).astype(jnp.bfloat16)
        key_rows = gsk[:, :, cols].reshape(total, PAIR)
        values = gsv[:, :, cols].reshape(total, PAIR)
        parts = []
        for h in (0, 1):
            top, own_mass, mixed = weigh(united * keep[h], key_rows, values, self_bias)
            parts.append(mixed / own_mass)
        attended = jnp.where(low, parts[0], parts[1])
        aout[:, cols] = jnp.where(audio_live, cross + attended, 0.0).astype(jnp.bfloat16)

    def drain(r, carry):
        for t in (Q, K, V, SK, SV):
            sent(t, r)
        for d in (0, 1):
            ahead = r > me if d == 0 else r < me

            @pl.when(ahead)
            def _():
                for c in pushes(d, r):
                    c.wait_send()

        return carry

    lax.fori_loop(0, n, drain, 0)


def solution(mesh):
    n = mesh.shape["seq"]

    def shards(*arrays):
        vslots, width = arrays[0].shape
        aslots = arrays[3].shape[0]
        frames = arrays[11].shape[0]
        smem = pl.BlockSpec(memory_space=pltpu.SMEM)
        anywhere = pl.BlockSpec(memory_space=pl.ANY)
        vmem = pl.BlockSpec(memory_space=pltpu.VMEM)
        half, full = jnp.bfloat16, jnp.float32
        return pl.pallas_call(
            functools.partial(kernel, n, frames),
            name="attend",
            out_shape=(
                jax.ShapeDtypeStruct((vslots, width), half),
                jax.ShapeDtypeStruct((aslots, width), half),
            ),
            in_specs=[smem] * 4 + [anywhere] * 9,
            out_specs=(vmem, vmem),
            scratch_shapes=[pltpu.VMEM((vslots, width), half)] * 3
            + [pltpu.VMEM((aslots, width), half)]
            + [pltpu.VMEM((n, aslots, width), half)] * 5
            + [
                pltpu.VMEM((vslots, n * aslots), full),
                pltpu.VMEM((n, aslots, width), full),
                pltpu.VMEM((n, aslots, PAIR), full),
                pltpu.VMEM((n, aslots, width), half),
                pltpu.VMEM((2, n, aslots, width), half),
                pltpu.VMEM((2, n, aslots, PAIR), full),
                pltpu.SemaphoreType.DMA((9,)),
                pltpu.SemaphoreType.DMA((5, 2, n)),
                pltpu.SemaphoreType.DMA((5, 2, n + 1)),
                pltpu.SemaphoreType.DMA((2, 2, n)),
                pltpu.SemaphoreType.DMA((2, 2, n)),
            ],
            compiler_params=pltpu.CompilerParams(
                collective_id=0, has_side_effects=True, vmem_limit_bytes=56 << 20
            ),
        )(*arrays[9:], *arrays[:9])

    rows = P(("groups", "seq"), ("heads", "sub"))
    return jax.shard_map(
        shards,
        mesh=mesh,
        in_specs=(rows,) * 9 + (P("groups"),) * 4,
        out_specs=(rows, rows),
        check_vma=False,
    )
```

```python
import functools
import math

import jax
import jax.numpy as jnp
from jax import lax
from jax.experimental import pallas as pl
from jax.experimental.pallas import tpu as pltpu
from jax.sharding import PartitionSpec as P

HD = 64
PAIR = 128
FRAME_TOKENS = 256
AUDIO_WIN_BLOCK = 128
NEG = -1e30
FAR = 1 << 20
SCALE = HD ** (-0.5) * math.log2(math.e)
MESH = pl.DeviceIdType.MESH
Q, K, V, SK, SV = range(5)


def kernel(
    n,
    frames,
    vcount,
    acount,
    wstart,
    wend,
    vq,
    vk,
    vv,
    aq,
    ak,
    av,
    sq,
    sk,
    sv,
    vout,
    aout,
    vqs,
    vks,
    vvs,
    sqs,
    gq,
    gk,
    gv,
    gsk,
    gsv,
    vbias,
    pacc,
    pst,
    sacc,
    racc,
    rst,
    local_sem,
    send_sem,
    recv_sem,
    psend,
    precv,
):
    me = lax.axis_index("seq")
    vslots, width = vqs.shape
    aslots = sqs.shape[0]
    pairs = width // PAIR
    total = n * aslots
    bufs = (gq, gk, gv, gsk, gsv)
    owns = (aq, ak, av, sk, sv)

    fetches = []
    for t in (Q, K, V, SK, SV):
        fetches.append(pltpu.make_async_copy(owns[t], bufs[t].at[me], local_sem.at[t]))
    for i, (a, b) in enumerate(((vk, vks), (vv, vvs), (vq, vqs), (sq, sqs))):
        fetches.append(pltpu.make_async_copy(a, b, local_sem.at[5 + i]))
    for f in fetches:
        f.start()

    has_left = me > 0
    has_right = me < n - 1
    barrier = pltpu.get_barrier_semaphore()

    @pl.when(has_left)
    def _():
        pl.semaphore_signal(barrier, inc=1, device_id={"seq": me - 1}, device_id_type=MESH)

    @pl.when(has_right)
    def _():
        pl.semaphore_signal(barrier, inc=1, device_id={"seq": me + 1}, device_id_type=MESH)

    @pl.when(jnp.logical_and(has_left, has_right))
    def _():
        pl.semaphore_wait(barrier, 2)

    @pl.when(jnp.logical_not(jnp.logical_and(has_left, has_right)))
    def _():
        pl.semaphore_wait(barrier, 1)

    def relay(t, d, r):
        source = me - r if d == 0 else me + r
        target = me + 1 if d == 0 else me - 1
        return pltpu.make_async_remote_copy(
            src_ref=bufs[t].at[source],
            dst_ref=bufs[t].at[source],
            send_sem=send_sem.at[t, d, r],
            recv_sem=recv_sem.at[t, d, r + 1],
            device_id={"seq": target},
            device_id_type=MESH,
        )

    def have(d, r):
        return me - r >= 0 if d == 0 else me + r <= n - 1

    def passes(d):
        return has_right if d == 0 else has_left

    def arrived(t, d, r):
        source = me - r if d == 0 else me + r
        pltpu.make_async_copy(
            bufs[t].at[source], bufs[t].at[source], recv_sem.at[t, d, r]
        ).wait()

    def forward(t, r, first=False):
        for d in (0, 1):

            @pl.when(have(d, r))
            def _():
                if not first:
                    arrived(t, d, r)

                @pl.when(passes(d))
                def _():
                    relay(t, d, r).start()

    def sent(t, r):
        for d in (0, 1):

            @pl.when(jnp.logical_and(have(d, r), passes(d)))
            def _():
                relay(t, d, r).wait_send()

    for t in (Q, K, V):
        fetches[t].wait()
        forward(t, 0, True)

    lane = lax.broadcasted_iota(jnp.int32, (1, PAIR), 1)
    low = lane < HD
    keep = (
        jnp.where(low, 1.0, 0.0).astype(jnp.bfloat16),
        jnp.where(low, 0.0, 1.0).astype(jnp.bfloat16),
    )

    def start_of(counts, index):
        at = jnp.int32(0)
        for s in range(n):
            at = at + jnp.where(s < index, counts[s], 0)
        return at

    def video_window(place):
        position = start_of(vcount, me) + place
        live = place < vcount[me]
        frame = position // FRAME_TOKENS
        first = jnp.full(place.shape, FAR, jnp.int32)
        final = jnp.zeros(place.shape, jnp.int32)
        for f in range(frames):
            here = jnp.logical_and(frame == f, live)
            first = jnp.where(here, wstart[f], first)
            final = jnp.where(here, wend[f], final)
        return first, final

    def weigh(query, key_rows, values, bias):
        rows = query.shape[0]
        both = jnp.concatenate([query * keep[0], query * keep[1]], axis=0)
        score = lax.dot_general(
            both, key_rows, (((1,), (1,)), ((), ())), preferred_element_type=jnp.float32
        )
        score = score.reshape(2, rows, key_rows.shape[0]) * SCALE + bias[None]
        top = jnp.max(score, axis=2, keepdims=True)
        weight = jnp.exp2(score - top)
        mass = jnp.sum(weight, axis=2, keepdims=True)
        mixed = jnp.dot(
            weight.astype(jnp.bfloat16).reshape(2 * rows, key_rows.shape[0]),
            values,
            preferred_element_type=jnp.float32,
        )
        return top, mass, jnp.where(low, mixed[:rows], mixed[rows:])

    first_row, final_row = video_window(lax.broadcasted_iota(jnp.int32, (1, vslots), 1))
    video_place = lax.broadcasted_iota(jnp.int32, (vslots, 1), 0)
    first_col, final_col = video_window(video_place)
    audio_index = lax.broadcasted_iota(jnp.int32, (1, total), 1)
    audio_block = jnp.full((1, total), -1, jnp.int32)
    begin = jnp.int32(0)
    for s in range(n):
        place = audio_index - s * aslots
        here = jnp.logical_and(place >= 0, place < acount[s])
        audio_block = jnp.where(here, (begin + place) // AUDIO_WIN_BLOCK, audio_block)
        begin = begin + acount[s]
    vbias[...] = jnp.where(
        jnp.logical_and(first_col <= audio_block, audio_block < final_col), 0.0, NEG
    )
    self_bias = jnp.where(audio_block >= 0, 0.0, NEG)
    audio_place = lax.broadcasted_iota(jnp.int32, (aslots, 1), 0)

    def columns(p):
        return pl.ds(pl.multiple_of(p * PAIR, PAIR), PAIR)

    def audio_cross(j):
        block = jnp.where(
            audio_place < acount[j],
            (start_of(acount, j) + audio_place) // AUDIO_WIN_BLOCK,
            -1,
        )
        bias = jnp.where(
            jnp.logical_and(first_row <= block, block < final_row), 0.0, NEG
        )

        def step(p, stats):
            cols = columns(p)
            query = gq[j, :, cols]
            key_rows = vks[:, cols]
            values = vvs[:, cols]
            top, mass, mixed = weigh(query, key_rows, values, bias)
            for h in (0, 1):
                stats = jnp.where(lane == 2 * p + h, top[h], stats)
                stats = jnp.where(lane == HD + 2 * p + h, mass[h], stats)
            pacc[j, :, cols] = mixed
            return stats

        pst[j] = lax.fori_loop(
            0, pairs, step, jnp.zeros((aslots, PAIR), jnp.float32), unroll=min(4, pairs)
        )

    fetches[5].wait()
    fetches[6].wait()

    def first_round(r, carry):
        @pl.when(r > 0)
        def _():
            for t in (Q, K, V):
                forward(t, r)

        @pl.when(have(0, r))
        def _():
            audio_cross(me - r)

        @pl.when(jnp.logical_and(have(1, r), r > 0))
        def _():
            audio_cross(me + r)

        return carry

    lax.fori_loop(0, n, first_round, 0)
    fetches[SK].wait()
    fetches[SV].wait()
    fetches[7].wait()
    fetches[8].wait()

    def merge(d, j):
        mine = pst[j]
        other = rst[d, j]
        top = jnp.maximum(mine, other)
        a = jnp.exp2(mine - top)
        b = jnp.exp2(other - top)
        mass = mine * pltpu.roll(a, HD, 1) + other * pltpu.roll(b, HD, 1)
        pst[j] = jnp.where(low, top, mass)
        for p in range(pairs):
            cols = pl.ds(p * PAIR, PAIR)
            wa = jnp.where(low, a[:, 2 * p : 2 * p + 1], a[:, 2 * p + 1 : 2 * p + 2])
            wb = jnp.where(low, b[:, 2 * p : 2 * p + 1], b[:, 2 * p + 1 : 2 * p + 2])
            pacc[j, :, cols] = pacc[j, :, cols] * wa + racc[d, j, :, cols].astype(
                jnp.float32
            ) * wb

    def pushes(d, j):
        target = me + 1 if d == 0 else me - 1
        return [
            pltpu.make_async_remote_copy(
                src_ref=src.at[j],
                dst_ref=dst.at[d, j],
                send_sem=psend.at[d, i, j],
                recv_sem=precv.at[d, i, j],
                device_id={"seq": target},
                device_id_type=MESH,
            )
            for i, (src, dst) in enumerate(((sacc, racc), (pst, rst)))
        ]

    def chain(d, step):
        lag = me if d == 0 else n - 1 - me
        j = n - 1 - step + me if d == 0 else step - (n - 1 - me)

        @pl.when(step >= lag)
        def _():
            @pl.when(passes(1 - d))
            def _():
                for i, dst in enumerate((racc, rst)):
                    pltpu.make_async_copy(
                        dst.at[d, j], dst.at[d, j], precv.at[d, i, j]
                    ).wait()
                merge(d, j)

            @pl.when(j != me)
            def _():
                sacc[j] = pacc[j].astype(jnp.bfloat16)
                for c in pushes(d, j):
                    c.start()

    video_live = video_place < vcount[me]
    chunk = 160 if vslots % 160 == 0 else vslots

    def video_pair(p, carry):
        cols = columns(p)
        key_rows = gk[:, :, cols].reshape(total, PAIR)
        values = gv[:, :, cols].reshape(total, PAIR)
        for c in range(vslots // chunk):
            rows = pl.ds(c * chunk, chunk)
            query = vqs[rows, cols]
            bias = vbias[rows, :]
            top, mass, mixed = weigh(query, key_rows, values, bias)
            result = mixed / jnp.where(low, mass[0], mass[1])
            live = video_live[c * chunk : (c + 1) * chunk]
            vout[rows, cols] = jnp.where(live, result, 0.0).astype(jnp.bfloat16)
        return carry

    per_step = -(-pairs // n)

    def second_round(r, carry):
        @pl.when(r == 0)
        def _():
            forward(SK, 0, True)
            forward(SV, 0, True)

        @pl.when(r > 0)
        def _():
            forward(SK, r)
            forward(SV, r)

        chain(0, r)
        chain(1, r)
        for i in range(per_step):

            @pl.when(r * per_step + i < pairs)
            def _():
                video_pair(r * per_step + i, 0)

        return carry

    lax.fori_loop(0, n, second_round, 0)

    audio_live = audio_place < acount[me]
    stats = pst[me]
    for p in range(pairs):
        cols = pl.ds(p * PAIR, PAIR)
        mass = jnp.where(
            low,
            stats[:, HD + 2 * p : HD + 2 * p + 1],
            stats[:, HD + 2 * p + 1 : HD + 2 * p + 2],
        )
        cross = jnp.where(audio_live, pacc[me, :, cols] / mass, 0.0)
        united = (sqs[:, cols].astype(jnp.float32) + cross).astype(jnp.bfloat16)
        key_rows = gsk[:, :, cols].reshape(total, PAIR)
        values = gsv[:, :, cols].reshape(total, PAIR)
        top, own_mass, mixed = weigh(united, key_rows, values, self_bias)
        attended = mixed / jnp.where(low, own_mass[0], own_mass[1])
        aout[:, cols] = jnp.where(audio_live, cross + attended, 0.0).astype(jnp.bfloat16)

    def drain(r, carry):
        for t in (Q, K, V, SK, SV):
            sent(t, r)
        for d in (0, 1):
            ahead = r > me if d == 0 else r < me

            @pl.when(ahead)
            def _():
                for c in pushes(d, r):
                    c.wait_send()

        return carry

    lax.fori_loop(0, n, drain, 0)


def solution(mesh):
    n = mesh.shape["seq"]

    def shards(*arrays):
        vslots, width = arrays[0].shape
        aslots = arrays[3].shape[0]
        frames = arrays[11].shape[0]
        smem = pl.BlockSpec(memory_space=pltpu.SMEM)
        anywhere = pl.BlockSpec(memory_space=pl.ANY)
        vmem = pl.BlockSpec(memory_space=pltpu.VMEM)
        half, full = jnp.bfloat16, jnp.float32
        return pl.pallas_call(
            functools.partial(kernel, n, frames),
            name="attend",
            out_shape=(
                jax.ShapeDtypeStruct((vslots, width), half),
                jax.ShapeDtypeStruct((aslots, width), half),
            ),
            in_specs=[smem] * 4 + [anywhere] * 9,
            out_specs=(vmem, vmem),
            scratch_shapes=[pltpu.VMEM((vslots, width), half)] * 3
            + [pltpu.VMEM((aslots, width), half)]
            + [pltpu.VMEM((n, aslots, width), half)] * 5
            + [
                pltpu.VMEM((vslots, n * aslots), full),
                pltpu.VMEM((n, aslots, width), full),
                pltpu.VMEM((n, aslots, PAIR), full),
                pltpu.VMEM((n, aslots, width), half),
                pltpu.VMEM((2, n, aslots, width), half),
                pltpu.VMEM((2, n, aslots, PAIR), full),
                pltpu.SemaphoreType.DMA((9,)),
                pltpu.SemaphoreType.DMA((5, 2, n)),
                pltpu.SemaphoreType.DMA((5, 2, n + 1)),
                pltpu.SemaphoreType.DMA((2, 2, n)),
                pltpu.SemaphoreType.DMA((2, 2, n)),
            ],
            compiler_params=pltpu.CompilerParams(
                collective_id=0, has_side_effects=True, vmem_limit_bytes=56 << 20
            ),
        )(*arrays[9:], *arrays[:9])

    rows = P(("groups", "seq"), ("heads", "sub"))
    return jax.shard_map(
        shards,
        mesh=mesh,
        in_specs=(rows,) * 9 + (P("groups"),) * 4,
        out_specs=(rows, rows),
        check_vma=False,
    )
```

```python
import functools
import math

import jax
import jax.numpy as jnp
from jax import lax
from jax.experimental import pallas as pl
from jax.experimental.pallas import tpu as pltpu
from jax.sharding import PartitionSpec as P

HD = 64
PAIR = 128
FRAME_TOKENS = 256
AUDIO_WIN_BLOCK = 128
NEG = -1e30
FAR = 1 << 20
SCALE = HD ** (-0.5) * math.log2(math.e)
MESH = pl.DeviceIdType.MESH
Q, K, V, SK, SV = range(5)


def kernel(
    n,
    frames,
    vcount,
    acount,
    wstart,
    wend,
    vq,
    vk,
    vv,
    aq,
    ak,
    av,
    sq,
    sk,
    sv,
    vout,
    aout,
    vqs,
    vks,
    vvs,
    sqs,
    gq,
    gk,
    gv,
    gsk,
    gsv,
    vbias,
    pacc,
    pst,
    sacc,
    racc,
    rst,
    local_sem,
    send_sem,
    recv_sem,
    psend,
    precv,
):
    me = lax.axis_index("seq")
    vslots, width = vqs.shape
    aslots = sqs.shape[0]
    pairs = width // PAIR
    total = n * aslots
    bufs = (gq, gk, gv, gsk, gsv)
    owns = (aq, ak, av, sk, sv)

    fetches = []
    for t in (Q, K, V, SK, SV):
        fetches.append(pltpu.make_async_copy(owns[t], bufs[t].at[me], local_sem.at[t]))
    for i, (a, b) in enumerate(((vk, vks), (vv, vvs), (vq, vqs), (sq, sqs))):
        fetches.append(pltpu.make_async_copy(a, b, local_sem.at[5 + i]))
    for f in fetches:
        f.start()

    has_left = me > 0
    has_right = me < n - 1
    barrier = pltpu.get_barrier_semaphore()

    @pl.when(has_left)
    def _():
        pl.semaphore_signal(barrier, inc=1, device_id={"seq": me - 1}, device_id_type=MESH)

    @pl.when(has_right)
    def _():
        pl.semaphore_signal(barrier, inc=1, device_id={"seq": me + 1}, device_id_type=MESH)

    @pl.when(jnp.logical_and(has_left, has_right))
    def _():
        pl.semaphore_wait(barrier, 2)

    @pl.when(jnp.logical_not(jnp.logical_and(has_left, has_right)))
    def _():
        pl.semaphore_wait(barrier, 1)

    def relay(t, d, r):
        source = me - r if d == 0 else me + r
        target = me + 1 if d == 0 else me - 1
        return pltpu.make_async_remote_copy(
            src_ref=bufs[t].at[source],
            dst_ref=bufs[t].at[source],
            send_sem=send_sem.at[t, d, r],
            recv_sem=recv_sem.at[t, d, r + 1],
            device_id={"seq": target},
            device_id_type=MESH,
        )

    def have(d, r):
        return me - r >= 0 if d == 0 else me + r <= n - 1

    def passes(d):
        return has_right if d == 0 else has_left

    def arrived(t, d, r):
        source = me - r if d == 0 else me + r
        pltpu.make_async_copy(
            bufs[t].at[source], bufs[t].at[source], recv_sem.at[t, d, r]
        ).wait()

    def forward(t, r, first=False):
        for d in (0, 1):

            @pl.when(have(d, r))
            def _():
                if not first:
                    arrived(t, d, r)

                @pl.when(passes(d))
                def _():
                    relay(t, d, r).start()

    def sent(t, r):
        for d in (0, 1):

            @pl.when(jnp.logical_and(have(d, r), passes(d)))
            def _():
                relay(t, d, r).wait_send()

    for t in (Q, K, V):
        fetches[t].wait()
        forward(t, 0, True)

    lane = lax.broadcasted_iota(jnp.int32, (1, PAIR), 1)
    low = lane < HD
    keep = (
        jnp.where(low, 1.0, 0.0).astype(jnp.bfloat16),
        jnp.where(low, 0.0, 1.0).astype(jnp.bfloat16),
    )

    def start_of(counts, index):
        at = jnp.int32(0)
        for s in range(n):
            at = at + jnp.where(s < index, counts[s], 0)
        return at

    def video_window(place):
        position = start_of(vcount, me) + place
        live = place < vcount[me]
        frame = position // FRAME_TOKENS
        first = jnp.full(place.shape, FAR, jnp.int32)
        final = jnp.zeros(place.shape, jnp.int32)
        for f in range(frames):
            here = jnp.logical_and(frame == f, live)
            first = jnp.where(here, wstart[f], first)
            final = jnp.where(here, wend[f], final)
        return first, final

    def weigh(query, key_rows, values, bias):
        rows = query.shape[0]
        both = jnp.concatenate([query * keep[0], query * keep[1]], axis=0)
        score = lax.dot_general(
            both, key_rows, (((1,), (1,)), ((), ())), preferred_element_type=jnp.float32
        )
        score = score.reshape(2, rows, key_rows.shape[0]) * SCALE + bias[None]
        top = jnp.max(score, axis=2, keepdims=True)
        weight = jnp.exp2(score - top)
        mass = jnp.sum(weight, axis=2, keepdims=True)
        mixed = jnp.dot(
            weight.astype(jnp.bfloat16).reshape(2 * rows, key_rows.shape[0]),
            values,
            preferred_element_type=jnp.float32,
        )
        return top, mass, jnp.where(low, mixed[:rows], mixed[rows:])

    first_row, final_row = video_window(lax.broadcasted_iota(jnp.int32, (1, vslots), 1))
    video_place = lax.broadcasted_iota(jnp.int32, (vslots, 1), 0)
    first_col, final_col = video_window(video_place)
    audio_index = lax.broadcasted_iota(jnp.int32, (1, total), 1)
    audio_block = jnp.full((1, total), -1, jnp.int32)
    begin = jnp.int32(0)
    for s in range(n):
        place = audio_index - s * aslots
        here = jnp.logical_and(place >= 0, place < acount[s])
        audio_block = jnp.where(here, (begin + place) // AUDIO_WIN_BLOCK, audio_block)
        begin = begin + acount[s]
    vbias[...] = jnp.where(
        jnp.logical_and(first_col <= audio_block, audio_block < final_col), 0.0, NEG
    )
    self_bias = jnp.where(audio_block >= 0, 0.0, NEG)
    audio_place = lax.broadcasted_iota(jnp.int32, (aslots, 1), 0)

    def columns(p):
        return pl.ds(pl.multiple_of(p * PAIR, PAIR), PAIR)

    def audio_cross(j):
        block = jnp.where(
            audio_place < acount[j],
            (start_of(acount, j) + audio_place) // AUDIO_WIN_BLOCK,
            -1,
        )
        bias = jnp.where(
            jnp.logical_and(first_row <= block, block < final_row), 0.0, NEG
        )

        def step(p, stats):
            cols = columns(p)
            query = gq[j, :, cols]
            key_rows = vks[:, cols]
            values = vvs[:, cols]
            top, mass, mixed = weigh(query, key_rows, values, bias)
            for h in (0, 1):
                stats = jnp.where(lane == 2 * p + h, top[h], stats)
                stats = jnp.where(lane == HD + 2 * p + h, mass[h], stats)
            pacc[j, :, cols] = mixed
            return stats

        pst[j] = lax.fori_loop(
            0, pairs, step, jnp.zeros((aslots, PAIR), jnp.float32), unroll=min(4, pairs)
        )

    fetches[5].wait()
    fetches[6].wait()
    fetches[SK].wait()
    fetches[SV].wait()
    early = n // 2 + 1 if n > 2 else n - 1

    def first_round(r, carry):
        @pl.when(r > 0)
        def _():
            forward(Q, r)

        @pl.when(have(0, r))
        def _():
            audio_cross(me - r)

        @pl.when(r > 0)
        def _():
            forward(K, r)
            forward(V, r)

        @pl.when(r == early)
        def _():
            forward(SK, 0, True)
            forward(SV, 0, True)

        @pl.when(r > early)
        def _():
            forward(SK, r - early)
            forward(SV, r - early)

        @pl.when(jnp.logical_and(have(1, r), r > 0))
        def _():
            audio_cross(me + r)

        return carry

    lax.fori_loop(0, n, first_round, 0)
    fetches[7].wait()
    fetches[8].wait()

    halves = 2 if pairs % 2 == 0 else 1
    half_pairs = pairs // halves

    def piece(h):
        return pl.ds(h * half_pairs * PAIR, half_pairs * PAIR)

    def push(d, i, j):
        target = me + 1 if d == 0 else me - 1
        if i == 0:
            src, dst = pst.at[j], rst.at[d, j]
        else:
            src, dst = sacc.at[j, :, piece(i - 1)], racc.at[d, j, :, piece(i - 1)]
        return pltpu.make_async_remote_copy(
            src_ref=src,
            dst_ref=dst,
            send_sem=psend.at[d, i, j],
            recv_sem=precv.at[d, i, j],
            device_id={"seq": target},
            device_id_type=MESH,
        )

    def landed(d, i, j):
        dst = rst.at[d, j] if i == 0 else racc.at[d, j, :, piece(i - 1)]
        pltpu.make_async_copy(dst, dst, precv.at[d, i, j]).wait()

    def chain(d, step):
        lag = me if d == 0 else n - 1 - me
        j = n - 1 - step + me if d == 0 else step - (n - 1 - me)
        receives = passes(1 - d)
        moves_on = j != me

        @pl.when(jnp.logical_and(step >= lag, jnp.logical_and(moves_on, jnp.logical_not(receives))))
        def _():
            push(d, 0, j).start()
            for h in range(halves):
                sacc[j, :, piece(h)] = pacc[j, :, piece(h)].astype(jnp.bfloat16)
                push(d, h + 1, j).start()

        @pl.when(jnp.logical_and(step >= lag, receives))
        def _():
            landed(d, 0, j)
            mine = pst[j]
            other = rst[d, j]
            top = jnp.maximum(mine, other)
            a = jnp.exp2(mine - top)
            b = jnp.exp2(other - top)
            mass = mine * pltpu.roll(a, HD, 1) + other * pltpu.roll(b, HD, 1)
            pst[j] = jnp.where(low, top, mass)

            @pl.when(moves_on)
            def _():
                push(d, 0, j).start()

            for h in range(halves):
                landed(d, h + 1, j)
                for p in range(h * half_pairs, (h + 1) * half_pairs):
                    cols = pl.ds(p * PAIR, PAIR)
                    wa = jnp.where(low, a[:, 2 * p : 2 * p + 1], a[:, 2 * p + 1 : 2 * p + 2])
                    wb = jnp.where(low, b[:, 2 * p : 2 * p + 1], b[:, 2 * p + 1 : 2 * p + 2])
                    merged = pacc[j, :, cols] * wa + racc[d, j, :, cols].astype(jnp.float32) * wb
                    pacc[j, :, cols] = merged
                    sacc[j, :, cols] = merged.astype(jnp.bfloat16)

                @pl.when(moves_on)
                def _():
                    push(d, h + 1, j).start()

    video_live = video_place < vcount[me]
    chunk = 160 if vslots % 160 == 0 else vslots

    def video_pair(p, carry):
        cols = columns(p)
        key_rows = gk[:, :, cols].reshape(total, PAIR)
        values = gv[:, :, cols].reshape(total, PAIR)
        for c in range(vslots // chunk):
            rows = pl.ds(c * chunk, chunk)
            query = vqs[rows, cols]
            bias = vbias[rows, :]
            top, mass, mixed = weigh(query, key_rows, values, bias)
            result = mixed / jnp.where(low, mass[0], mass[1])
            live = video_live[c * chunk : (c + 1) * chunk]
            vout[rows, cols] = jnp.where(live, result, 0.0).astype(jnp.bfloat16)
        return carry

    per_step = -(-pairs // n)

    def second_round(r, carry):
        @pl.when(r < early)
        def _():
            forward(SK, r + n - early)
            forward(SV, r + n - early)

        chain(0, r)
        chain(1, r)
        for i in range(per_step):

            @pl.when(r * per_step + i < pairs)
            def _():
                video_pair(r * per_step + i, 0)

        return carry

    lax.fori_loop(0, n, second_round, 0)

    audio_live = audio_place < acount[me]
    stats = pst[me]
    for p in range(pairs):
        cols = pl.ds(p * PAIR, PAIR)
        mass = jnp.where(
            low,
            stats[:, HD + 2 * p : HD + 2 * p + 1],
            stats[:, HD + 2 * p + 1 : HD + 2 * p + 2],
        )
        cross = jnp.where(audio_live, pacc[me, :, cols] / mass, 0.0)
        united = (sqs[:, cols].astype(jnp.float32) + cross).astype(jnp.bfloat16)
        key_rows = gsk[:, :, cols].reshape(total, PAIR)
        values = gsv[:, :, cols].reshape(total, PAIR)
        top, own_mass, mixed = weigh(united, key_rows, values, self_bias)
        attended = mixed / jnp.where(low, own_mass[0], own_mass[1])
        aout[:, cols] = jnp.where(audio_live, cross + attended, 0.0).astype(jnp.bfloat16)

    def drain(r, carry):
        for t in (Q, K, V, SK, SV):
            sent(t, r)
        for d in (0, 1):
            ahead = r > me if d == 0 else r < me

            @pl.when(ahead)
            def _():
                for i in range(halves + 1):
                    push(d, i, r).wait_send()

        return carry

    lax.fori_loop(0, n, drain, 0)


def solution(mesh):
    n = mesh.shape["seq"]

    def shards(*arrays):
        vslots, width = arrays[0].shape
        aslots = arrays[3].shape[0]
        frames = arrays[11].shape[0]
        smem = pl.BlockSpec(memory_space=pltpu.SMEM)
        anywhere = pl.BlockSpec(memory_space=pl.ANY)
        vmem = pl.BlockSpec(memory_space=pltpu.VMEM)
        half, full = jnp.bfloat16, jnp.float32
        return pl.pallas_call(
            functools.partial(kernel, n, frames),
            name="attend",
            out_shape=(
                jax.ShapeDtypeStruct((vslots, width), half),
                jax.ShapeDtypeStruct((aslots, width), half),
            ),
            in_specs=[smem] * 4 + [anywhere] * 9,
            out_specs=(vmem, vmem),
            scratch_shapes=[pltpu.VMEM((vslots, width), half)] * 3
            + [pltpu.VMEM((aslots, width), half)]
            + [pltpu.VMEM((n, aslots, width), half)] * 5
            + [
                pltpu.VMEM((vslots, n * aslots), full),
                pltpu.VMEM((n, aslots, width), full),
                pltpu.VMEM((n, aslots, PAIR), full),
                pltpu.VMEM((n, aslots, width), half),
                pltpu.VMEM((2, n, aslots, width), half),
                pltpu.VMEM((2, n, aslots, PAIR), full),
                pltpu.SemaphoreType.DMA((9,)),
                pltpu.SemaphoreType.DMA((5, 2, n)),
                pltpu.SemaphoreType.DMA((5, 2, n + 1)),
                pltpu.SemaphoreType.DMA((2, 3, n)),
                pltpu.SemaphoreType.DMA((2, 3, n)),
            ],
            compiler_params=pltpu.CompilerParams(
                collective_id=0, has_side_effects=True, vmem_limit_bytes=56 << 20
            ),
        )(*arrays[9:], *arrays[:9])

    rows = P(("groups", "seq"), ("heads", "sub"))
    return jax.shard_map(
        shards,
        mesh=mesh,
        in_specs=(rows,) * 9 + (P("groups"),) * 4,
        out_specs=(rows, rows),
        check_vma=False,
    )
```

```python
import functools
import math

import jax
import jax.numpy as jnp
from jax import lax
from jax.experimental import pallas as pl
from jax.experimental.pallas import tpu as pltpu
from jax.sharding import PartitionSpec as P

HD = 64
PAIR = 128
FRAME_TOKENS = 256
AUDIO_WIN_BLOCK = 128
NEG = -1e30
FAR = 1 << 20
SCALE = HD ** (-0.5) * math.log2(math.e)
MESH = pl.DeviceIdType.MESH
Q, K, V, SK, SV = range(5)


def kernel(
    n,
    frames,
    vcount,
    acount,
    wstart,
    wend,
    vq,
    vk,
    vv,
    aq,
    ak,
    av,
    sq,
    sk,
    sv,
    vout,
    aout,
    vqs,
    vks,
    vvs,
    sqs,
    gq,
    gk,
    gv,
    gsk,
    gsv,
    vbias,
    pacc,
    pst,
    sacc,
    racc,
    rst,
    local_sem,
    send_sem,
    recv_sem,
    psend,
    precv,
):
    me = lax.axis_index("seq")
    vslots, width = vqs.shape
    aslots = sqs.shape[0]
    pairs = width // PAIR
    total = n * aslots
    bufs = (gq, gk, gv, gsk, gsv)
    owns = (aq, ak, av, sk, sv)

    fetches = []
    for t in (Q, K, V, SK, SV):
        fetches.append(pltpu.make_async_copy(owns[t], bufs[t].at[me], local_sem.at[t]))
    for i, (a, b) in enumerate(((vk, vks), (vv, vvs), (vq, vqs), (sq, sqs))):
        fetches.append(pltpu.make_async_copy(a, b, local_sem.at[5 + i]))
    for f in fetches:
        f.start()

    has_left = me > 0
    has_right = me < n - 1
    barrier = pltpu.get_barrier_semaphore()

    @pl.when(has_left)
    def _():
        pl.semaphore_signal(barrier, inc=1, device_id={"seq": me - 1}, device_id_type=MESH)

    @pl.when(has_right)
    def _():
        pl.semaphore_signal(barrier, inc=1, device_id={"seq": me + 1}, device_id_type=MESH)

    @pl.when(jnp.logical_and(has_left, has_right))
    def _():
        pl.semaphore_wait(barrier, 2)

    @pl.when(jnp.logical_not(jnp.logical_and(has_left, has_right)))
    def _():
        pl.semaphore_wait(barrier, 1)

    def relay(t, d, r):
        source = me - r if d == 0 else me + r
        target = me + 1 if d == 0 else me - 1
        return pltpu.make_async_remote_copy(
            src_ref=bufs[t].at[source],
            dst_ref=bufs[t].at[source],
            send_sem=send_sem.at[t, d, r],
            recv_sem=recv_sem.at[t, d, r + 1],
            device_id={"seq": target},
            device_id_type=MESH,
        )

    def have(d, r):
        return me - r >= 0 if d == 0 else me + r <= n - 1

    def passes(d):
        return has_right if d == 0 else has_left

    def arrived(t, d, r):
        source = me - r if d == 0 else me + r
        pltpu.make_async_copy(
            bufs[t].at[source], bufs[t].at[source], recv_sem.at[t, d, r]
        ).wait()

    def forward(t, r, first=False):
        for d in (0, 1):

            @pl.when(have(d, r))
            def _():
                if not first:
                    arrived(t, d, r)

                @pl.when(passes(d))
                def _():
                    relay(t, d, r).start()

    def sent(t, r):
        for d in (0, 1):

            @pl.when(jnp.logical_and(have(d, r), passes(d)))
            def _():
                relay(t, d, r).wait_send()

    for t in (Q, K, V):
        fetches[t].wait()
        forward(t, 0, True)

    lane = lax.broadcasted_iota(jnp.int32, (1, PAIR), 1)
    low = lane < HD
    keep = (
        jnp.where(low, 1.0, 0.0).astype(jnp.bfloat16),
        jnp.where(low, 0.0, 1.0).astype(jnp.bfloat16),
    )

    def start_of(counts, index):
        at = jnp.int32(0)
        for s in range(n):
            at = at + jnp.where(s < index, counts[s], 0)
        return at

    def video_window(place):
        position = start_of(vcount, me) + place
        live = place < vcount[me]
        frame = position // FRAME_TOKENS
        first = jnp.full(place.shape, FAR, jnp.int32)
        final = jnp.zeros(place.shape, jnp.int32)
        for f in range(frames):
            here = jnp.logical_and(frame == f, live)
            first = jnp.where(here, wstart[f], first)
            final = jnp.where(here, wend[f], final)
        return first, final

    def weigh(query, key_rows, values, bias):
        rows = query.shape[0]
        both = jnp.concatenate([query * keep[0], query * keep[1]], axis=0)
        score = lax.dot_general(
            both, key_rows, (((1,), (1,)), ((), ())), preferred_element_type=jnp.float32
        )
        score = score.reshape(2, rows, key_rows.shape[0]) * SCALE + bias[None]
        top = jnp.max(score, axis=2, keepdims=True)
        weight = jnp.exp2(score - top)
        mass = jnp.sum(weight, axis=2, keepdims=True)
        mixed = jnp.dot(
            weight.astype(jnp.bfloat16).reshape(2 * rows, key_rows.shape[0]),
            values,
            preferred_element_type=jnp.float32,
        )
        return top, mass, jnp.where(low, mixed[:rows], mixed[rows:])

    first_row, final_row = video_window(lax.broadcasted_iota(jnp.int32, (1, vslots), 1))
    video_place = lax.broadcasted_iota(jnp.int32, (vslots, 1), 0)
    first_col, final_col = video_window(video_place)
    audio_index = lax.broadcasted_iota(jnp.int32, (1, total), 1)
    audio_block = jnp.full((1, total), -1, jnp.int32)
    begin = jnp.int32(0)
    for s in range(n):
        place = audio_index - s * aslots
        here = jnp.logical_and(place >= 0, place < acount[s])
        audio_block = jnp.where(here, (begin + place) // AUDIO_WIN_BLOCK, audio_block)
        begin = begin + acount[s]
    vbias[...] = jnp.where(
        jnp.logical_and(first_col <= audio_block, audio_block < final_col), 0.0, NEG
    )
    self_bias = jnp.where(audio_block >= 0, 0.0, NEG)
    audio_place = lax.broadcasted_iota(jnp.int32, (aslots, 1), 0)

    def columns(p):
        return pl.ds(pl.multiple_of(p * PAIR, PAIR), PAIR)

    def audio_cross(j):
        block = jnp.where(
            audio_place < acount[j],
            (start_of(acount, j) + audio_place) // AUDIO_WIN_BLOCK,
            -1,
        )
        bias = jnp.where(
            jnp.logical_and(first_row <= block, block < final_row), 0.0, NEG
        )

        def step(p, stats):
            cols = columns(p)
            query = gq[j, :, cols]
            key_rows = vks[:, cols]
            values = vvs[:, cols]
            top, mass, mixed = weigh(query, key_rows, values, bias)
            for h in (0, 1):
                stats = jnp.where(lane == 2 * p + h, top[h], stats)
                stats = jnp.where(lane == HD + 2 * p + h, mass[h], stats)
            pacc[j, :, cols] = mixed
            return stats

        pst[j] = lax.fori_loop(
            0, pairs, step, jnp.zeros((aslots, PAIR), jnp.float32), unroll=min(4, pairs)
        )

    fetches[5].wait()
    fetches[6].wait()
    fetches[SK].wait()
    fetches[SV].wait()
    early = n // 2 + 1 if n > 2 else n - 1

    def first_round(r, carry):
        @pl.when(r > 0)
        def _():
            forward(Q, r)

        @pl.when(have(0, r))
        def _():
            audio_cross(me - r)

        @pl.when(r > 0)
        def _():
            forward(K, r)
            forward(V, r)

        @pl.when(r == early)
        def _():
            forward(SK, 0, True)
            forward(SV, 0, True)

        @pl.when(r > early)
        def _():
            forward(SK, r - early)
            forward(SV, r - early)

        @pl.when(jnp.logical_and(have(1, r), r > 0))
        def _():
            audio_cross(me + r)

        return carry

    lax.fori_loop(0, n, first_round, 0)
    fetches[7].wait()
    fetches[8].wait()

    halves = 2 if pairs % 2 == 0 else 1
    half_pairs = pairs // halves

    def piece(h):
        return pl.ds(h * half_pairs * PAIR, half_pairs * PAIR)

    def push(d, i, j):
        target = me + 1 if d == 0 else me - 1
        if i == 0:
            src, dst = pst.at[j], rst.at[d, j]
        else:
            src, dst = sacc.at[j, :, piece(i - 1)], racc.at[d, j, :, piece(i - 1)]
        return pltpu.make_async_remote_copy(
            src_ref=src,
            dst_ref=dst,
            send_sem=psend.at[d, i, j],
            recv_sem=precv.at[d, i, j],
            device_id={"seq": target},
            device_id_type=MESH,
        )

    def landed(d, i, j):
        dst = rst.at[d, j] if i == 0 else racc.at[d, j, :, piece(i - 1)]
        pltpu.make_async_copy(dst, dst, precv.at[d, i, j]).wait()

    def chain(d, step):
        lag = me if d == 0 else n - 1 - me
        j = n - 1 - step + me if d == 0 else step - (n - 1 - me)
        receives = passes(1 - d)
        moves_on = j != me

        @pl.when(jnp.logical_and(step >= lag, jnp.logical_and(moves_on, jnp.logical_not(receives))))
        def _():
            push(d, 0, j).start()
            for h in range(halves):
                sacc[j, :, piece(h)] = pacc[j, :, piece(h)].astype(jnp.bfloat16)
                push(d, h + 1, j).start()

        @pl.when(jnp.logical_and(step >= lag, receives))
        def _():
            landed(d, 0, j)
            mine = pst[j]
            other = rst[d, j]
            top = jnp.maximum(mine, other)
            a = jnp.exp2(mine - top)
            b = jnp.exp2(other - top)
            mass = mine * pltpu.roll(a, HD, 1) + other * pltpu.roll(b, HD, 1)
            pst[j] = jnp.where(low, top, mass)

            @pl.when(moves_on)
            def _():
                push(d, 0, j).start()

            for h in range(halves):
                landed(d, h + 1, j)
                for p in range(h * half_pairs, (h + 1) * half_pairs):
                    cols = pl.ds(p * PAIR, PAIR)
                    wa = jnp.where(low, a[:, 2 * p : 2 * p + 1], a[:, 2 * p + 1 : 2 * p + 2])
                    wb = jnp.where(low, b[:, 2 * p : 2 * p + 1], b[:, 2 * p + 1 : 2 * p + 2])
                    merged = pacc[j, :, cols] * wa + racc[d, j, :, cols].astype(jnp.float32) * wb
                    pacc[j, :, cols] = merged
                    sacc[j, :, cols] = merged.astype(jnp.bfloat16)

                @pl.when(moves_on)
                def _():
                    push(d, h + 1, j).start()

    video_live = video_place < vcount[me]
    chunk = 160 if vslots % 160 == 0 else vslots

    def video_pair(p, carry):
        cols = columns(p)
        key_rows = gk[:, :, cols].reshape(total, PAIR)
        values = gv[:, :, cols].reshape(total, PAIR)
        for c in range(vslots // chunk):
            rows = pl.ds(c * chunk, chunk)
            query = vqs[rows, cols]
            bias = vbias[rows, :]
            top, mass, mixed = weigh(query, key_rows, values, bias)
            result = mixed / jnp.where(low, mass[0], mass[1])
            live = video_live[c * chunk : (c + 1) * chunk]
            vout[rows, cols] = jnp.where(live, result, 0.0).astype(jnp.bfloat16)
        return carry

    per_step = -(-pairs // n)

    def second_round(r, carry):
        chain(0, r)
        chain(1, r)

        @pl.when(r < early)
        def _():
            forward(SK, r + n - early)
            forward(SV, r + n - early)

        for i in range(per_step):

            @pl.when(r * per_step + i < pairs)
            def _():
                video_pair(r * per_step + i, 0)

        return carry

    lax.fori_loop(0, n, second_round, 0)

    audio_live = audio_place < acount[me]
    stats = pst[me]
    for p in range(pairs):
        cols = pl.ds(p * PAIR, PAIR)
        mass = jnp.where(
            low,
            stats[:, HD + 2 * p : HD + 2 * p + 1],
            stats[:, HD + 2 * p + 1 : HD + 2 * p + 2],
        )
        cross = jnp.where(audio_live, pacc[me, :, cols] / mass, 0.0)
        united = (sqs[:, cols].astype(jnp.float32) + cross).astype(jnp.bfloat16)
        key_rows = gsk[:, :, cols].reshape(total, PAIR)
        values = gsv[:, :, cols].reshape(total, PAIR)
        top, own_mass, mixed = weigh(united, key_rows, values, self_bias)
        attended = mixed / jnp.where(low, own_mass[0], own_mass[1])
        aout[:, cols] = jnp.where(audio_live, cross + attended, 0.0).astype(jnp.bfloat16)

    def drain(r, carry):
        for t in (Q, K, V, SK, SV):
            sent(t, r)
        for d in (0, 1):
            ahead = r > me if d == 0 else r < me

            @pl.when(ahead)
            def _():
                for i in range(halves + 1):
                    push(d, i, r).wait_send()

        return carry

    lax.fori_loop(0, n, drain, 0)


def solution(mesh):
    n = mesh.shape["seq"]

    def shards(*arrays):
        vslots, width = arrays[0].shape
        aslots = arrays[3].shape[0]
        frames = arrays[11].shape[0]
        smem = pl.BlockSpec(memory_space=pltpu.SMEM)
        anywhere = pl.BlockSpec(memory_space=pl.ANY)
        vmem = pl.BlockSpec(memory_space=pltpu.VMEM)
        half, full = jnp.bfloat16, jnp.float32
        return pl.pallas_call(
            functools.partial(kernel, n, frames),
            name="attend",
            out_shape=(
                jax.ShapeDtypeStruct((vslots, width), half),
                jax.ShapeDtypeStruct((aslots, width), half),
            ),
            in_specs=[smem] * 4 + [anywhere] * 9,
            out_specs=(vmem, vmem),
            scratch_shapes=[pltpu.VMEM((vslots, width), half)] * 3
            + [pltpu.VMEM((aslots, width), half)]
            + [pltpu.VMEM((n, aslots, width), half)] * 5
            + [
                pltpu.VMEM((vslots, n * aslots), full),
                pltpu.VMEM((n, aslots, width), full),
                pltpu.VMEM((n, aslots, PAIR), full),
                pltpu.VMEM((n, aslots, width), half),
                pltpu.VMEM((2, n, aslots, width), half),
                pltpu.VMEM((2, n, aslots, PAIR), full),
                pltpu.SemaphoreType.DMA((9,)),
                pltpu.SemaphoreType.DMA((5, 2, n)),
                pltpu.SemaphoreType.DMA((5, 2, n + 1)),
                pltpu.SemaphoreType.DMA((2, 3, n)),
                pltpu.SemaphoreType.DMA((2, 3, n)),
            ],
            compiler_params=pltpu.CompilerParams(
                collective_id=0, has_side_effects=True, vmem_limit_bytes=56 << 20
            ),
        )(*arrays[9:], *arrays[:9])

    rows = P(("groups", "seq"), ("heads", "sub"))
    return jax.shard_map(
        shards,
        mesh=mesh,
        in_specs=(rows,) * 9 + (P("groups"),) * 4,
        out_specs=(rows, rows),
        check_vma=False,
    )
```
